32 devices in a mesh: section: 4 (over x, core), dom: 8 (over z, y).
Axes of the slice: x: 2, y: 2, z: 4, core: 2. Of those that a mesh axis runs over, the one named last changes fastest.
Arguments:
- voltages: bfloat16 [512, 64, 2048], P('dom'), may hold values from -6 to 6
- station_map: int32 [512], replicated, may hold values from 0 to 511, each once
- beam_table: int32 [128, 512], replicated, may hold values from 0 to 63
- weight_table: bfloat16 [2, 64, 1024], P(None, None, 'dom'), may hold values from -0.3125 to 0.3125
- dm_trial: int32 [128], replicated, may hold values from 0 to 31
Outputs:
- power: float32 [128, 64, 1024], P(('section', 'dom'))
The draws below stay inside these ranges and needn't reach their ends.
Inputs may be any that keep to these rules, and one draw needn't show every extreme that they name: `station_map`: each of the 512 stations appears once.
All inputs are finite; a program needn't handle non-finite values.
Results may differ from the reference program's by a relative error of at most 0.0042.
Values may be sent and summed in bfloat16 or wider, within the bound.
A program may use at most 128 MiB of HBM per device.

```python
import math
import jax
import jax.numpy as jnp
from jax import lax

NSTAT = 512
NFFT = 2048
CH = 1024
BEAMS = 128
NTAB = 64
FRAMES = 64
NDM = 32


def place_ends(values, stream_key, smallest, largest):
    longest = values.shape.index(max(values.shape))
    spots = []
    for shift in (0, 1):
        where = [jax.random.randint(jax.random.fold_in(stream_key, axis), (), 0, length) for axis, length in enumerate(values.shape)]
        where[longest] = (where[longest] + shift) % values.shape[longest]
        spots.append(tuple(where))
    return values.at[spots[0]].set(smallest).at[spots[1]].set(largest)


def level_of(stream_key, dims, pieces, least, largest):
    factor_of, own = 1.0, jax.random.fold_in(stream_key, 6)
    for axis_at, blocks in pieces:
        heights = jnp.exp(jax.random.uniform(jax.random.fold_in(own, axis_at), (blocks,), jnp.float32, least / len(pieces), largest / len(pieces)))
        factor_of = factor_of * jnp.repeat(heights, dims[axis_at] // blocks).reshape([-1 if axis == axis_at else 1 for axis in range(len(dims))])
    return factor_of


def normal_values(rng, shape, scale, reach, cuts=(), kind=jnp.bfloat16):
    entries = scale * jax.random.normal(rng, shape, jnp.float32)
    if cuts:
        entries = entries * level_of(rng, shape, cuts, -0.22, 0.18)
    return jnp.clip(entries, -reach, reach).astype(kind)


def setup_inputs(seed: int = 0) -> dict:
    key_list = jax.random.split(jax.random.key(seed), 6)
    return {
        "voltages": normal_values(key_list[0], (NSTAT, FRAMES, NFFT), 1.0, 6.0, ((0, 8),)),
        "station_map": jax.random.permutation(key_list[1], NSTAT).astype(jnp.int32),
        "beam_table": place_ends(jax.random.randint(key_list[2], (BEAMS, NSTAT), 0, NTAB), jax.random.fold_in(key_list[2], 1), 0, NTAB - 1).astype(jnp.int32),
        "weight_table": normal_values(key_list[3], (2, NTAB, CH), (3 * NSTAT // 4) ** -0.5, 0.3125, ((2, 8),)),
        "dm_trial": place_ends(jax.random.randint(key_list[4], (BEAMS,), 0, NDM), jax.random.fold_in(key_list[4], 1), 0, NDM - 1).astype(jnp.int32),
    }


def dft_table():
    sample_index = jnp.arange(NFFT, dtype=jnp.int32)
    window = 0.5 - 0.5 * jnp.cos(sample_index.astype(jnp.float32) * (2.0 * math.pi / NFFT))
    column = jnp.arange(NFFT, dtype=jnp.int32)
    bin_index = column % CH
    product = sample_index[:, None] * bin_index[None, :] % NFFT
    angle = product.astype(jnp.float32) * (2.0 * math.pi / NFFT)
    values = jnp.where(column[None, :] < CH, jnp.cos(angle), -jnp.sin(angle))
    return (values * (window[:, None] / math.sqrt(NFFT))).astype(jnp.bfloat16)

def reference(voltages, station_map, beam_table, weight_table, dm_trial):
    table = dft_table()
    flat = voltages.reshape(NSTAT * FRAMES, NFFT)
    spectra = jnp.dot(flat, table, preferred_element_type=jnp.float32).reshape(NSTAT, FRAMES, NFFT)
    chan_re = spectra[:, :, :CH].astype(jnp.bfloat16)
    chan_im = spectra[:, :, CH:].astype(jnp.bfloat16)
    ordered = beam_table[:, station_map]
    block_size = min(64, CH)

    def form(block_index):
        start = (block_index * block_size).astype(jnp.int32)
        table_re = lax.dynamic_slice_in_dim(weight_table[0], start, block_size, 1)
        table_im = lax.dynamic_slice_in_dim(weight_table[1], start, block_size, 1)
        w_re = table_re[ordered].astype(jnp.float32)
        w_im = table_im[ordered].astype(jnp.float32)
        x_re = lax.dynamic_slice_in_dim(chan_re, start, block_size, 2).astype(jnp.float32)
        x_im = lax.dynamic_slice_in_dim(chan_im, start, block_size, 2).astype(jnp.float32)
        beam_re = jnp.einsum('bsc,sfc->bfc', w_re, x_re) - jnp.einsum('bsc,sfc->bfc', w_im, x_im)
        beam_im = jnp.einsum('bsc,sfc->bfc', w_re, x_im) + jnp.einsum('bsc,sfc->bfc', w_im, x_re)
        return (beam_re, beam_im)
    blocks_re, blocks_im = lax.map(form, jnp.arange(CH // block_size, dtype=jnp.int32))
    beams_re = jnp.transpose(blocks_re, (1, 2, 0, 3)).reshape(BEAMS, FRAMES, CH)
    beams_im = jnp.transpose(blocks_im, (1, 2, 0, 3)).reshape(BEAMS, FRAMES, CH)
    spectrum = jnp.fft.fft(beams_re + 1j * beams_im, axis=1)
    bins = jnp.arange(FRAMES, dtype=jnp.int32)
    kappa = jnp.where(bins < FRAMES // 2, bins, bins - FRAMES).astype(jnp.float32)
    freq = 1.0 + jnp.arange(CH, dtype=jnp.float32) / CH
    spread = 1.0 / (freq * freq * freq)
    measure = (dm_trial + 1).astype(jnp.float32) / NDM
    coeff = math.pi * measure[:, None] * spread[None, :]
    phase = coeff[:, None, :] * (kappa * kappa / FRAMES)[None, :, None]
    rotated = spectrum * (jnp.cos(phase) + 1j * jnp.sin(phase))
    series = jnp.fft.ifft(rotated, axis=1)
    power = jnp.real(series) * jnp.real(series) + jnp.imag(series) * jnp.imag(series)
    return power.astype(jnp.float32)
```

```python
import math

import jax
import jax.numpy as jnp
from jax import lax
from jax.experimental import pallas as pl
from jax.experimental.pallas import tpu as pltpu
from jax.sharding import PartitionSpec as P

NFFT = 2048
CH = 1024
NTAB = 64
NDM = 32
LANES = 128
TILE = 64


def phasor_rows(steps, channels):
    product = steps[:, None] * channels[None, :] % NFFT
    angle = product.astype(jnp.float32) * (2.0 * math.pi / NFFT)
    return jnp.cos(angle), jnp.sin(angle)


def dft_columns(channels, is_imag):
    fine = 64
    coarse = NFFT // fine
    cos_a, sin_a = phasor_rows(fine * jnp.arange(coarse, dtype=jnp.int32), channels)
    cos_b, sin_b = phasor_rows(jnp.arange(fine, dtype=jnp.int32), channels)
    first = jnp.where(is_imag[None, :], -sin_a, cos_a)
    second = jnp.where(is_imag[None, :], -cos_a, -sin_a)
    sample = jnp.arange(NFFT, dtype=jnp.int32).astype(jnp.float32)
    window = 0.5 - 0.5 * jnp.cos(sample * (2.0 * math.pi / NFFT))
    window = window.reshape(coarse, fine) / math.sqrt(NFFT)
    first, second, cos_b, sin_b, window = lax.optimization_barrier(
        (first, second, cos_b, sin_b, window)
    )
    values = first[:, None, :] * cos_b[None] + second[:, None, :] * sin_b[None]
    values = values * window[:, :, None]
    return values.astype(jnp.bfloat16).reshape(NFFT, channels.shape[0])


def split_bf16(values):
    high = lax.reduce_precision(values, 8, 7)
    return high.astype(jnp.bfloat16), (values - high).astype(jnp.bfloat16)


def frame_matrices(frames, sections, groups):
    index = jnp.arange(frames, dtype=jnp.int32)
    angle = (index[:, None] * index[None, :] % frames).astype(jnp.float32) * (
        2.0 * math.pi / frames
    )
    cosine = jnp.cos(angle)
    sine = jnp.sin(angle)
    local = frames // sections
    forward = jnp.stack((jnp.stack((cosine, sine), 1), jnp.stack((-sine, cosine), 1)), 0)
    forward = forward.reshape(2 * frames, 2, sections, local).transpose(0, 2, 1, 3)
    forward = jnp.broadcast_to(
        forward[:, :, None], (2 * frames, sections, groups, 2, local)
    ).reshape(2 * frames, groups * 2 * frames)
    inverse = jnp.stack((jnp.stack((cosine, -sine), 1), jnp.stack((sine, cosine), 1)), 0)
    inverse = inverse.reshape(2 * frames, 2 * frames) / frames
    return split_bf16(forward) + split_bf16(inverse)


def pick_lanes(entries, where):
    dims = lax.GatherDimensionNumbers(
        offset_dims=(),
        collapsed_slice_dims=(1,),
        start_index_map=(1,),
        operand_batching_dims=(0,),
        start_indices_batching_dims=(0,),
    )
    return lax.gather(
        entries,
        where[..., None],
        dims,
        slice_sizes=(1, 1),
        mode=lax.GatherScatterMode.PROMISE_IN_BOUNDS,
    )


def weight_kernel(table_ref, index_ref, out_ref):
    stations, beams = index_ref.shape
    count = table_ref.shape[0]
    for tile in range(stations // TILE):
        span = pl.ds(tile * TILE, TILE)
        real_at = index_ref[span, :]
        imag_at = real_at + NTAB
        for chan in range(count):
            entry = jnp.broadcast_to(table_ref[pl.ds(chan, 1), :], (TILE, LANES))
            for part, where in enumerate((real_at, imag_at)):
                picked = pick_lanes(entry, where)
                out_ref[chan, span, pl.ds(part * beams, beams)] = picked.astype(jnp.bfloat16)


def station_weights(table, index):
    stations, beams = index.shape
    chans = table.shape[0]
    block = min(8, chans)
    return pl.pallas_call(
        weight_kernel,
        grid=(chans // block,),
        in_specs=[
            pl.BlockSpec((block, LANES), lambda i: (i, 0)),
            pl.BlockSpec((stations, beams), lambda i: (0, 0)),
        ],
        out_specs=pl.BlockSpec((block, stations, 2 * beams), lambda i: (i, 0, 0)),
        out_shape=jax.ShapeDtypeStruct((chans, stations, 2 * beams), jnp.bfloat16),
        cost_estimate=pl.CostEstimate(
            flops=0, bytes_accessed=chans * 2 * beams * stations * 5, transcendentals=0
        ),
        name="station_weights",
    )(table, index)


def beam_kernel(signal_ref, weight_ref, out_ref):
    count, depth, _ = signal_ref.shape
    beams = out_ref.shape[2]
    half = depth // 2
    for chan in range(count):
        product = jnp.dot(
            signal_ref[chan], weight_ref[chan], preferred_element_type=jnp.float32
        )
        real = product[:half, :beams] - product[half:, beams:]
        imag = product[half:, :beams] + product[:half, beams:]
        out_ref[chan, :half] = real.astype(jnp.bfloat16)
        out_ref[chan, half:] = imag.astype(jnp.bfloat16)


def form_beams(signal, weights):
    chans, depth, held = signal.shape
    beams = weights.shape[2] // 2
    block = min(16, chans)
    return pl.pallas_call(
        beam_kernel,
        grid=(chans // block,),
        in_specs=[
            pl.BlockSpec((block, depth, held), lambda i: (i, 0, 0)),
            pl.BlockSpec((block, held, 2 * beams), lambda i: (i, 0, 0)),
        ],
        out_specs=pl.BlockSpec((block, depth, beams), lambda i: (i, 0, 0)),
        out_shape=jax.ShapeDtypeStruct((chans, depth, beams), jnp.bfloat16),
        cost_estimate=pl.CostEstimate(
            flops=chans * depth * held * beams * 4,
            bytes_accessed=chans * held * beams * 6,
            transcendentals=0,
        ),
        name="form_beams",
    )(signal, weights)


def dedisperse_kernel(x_ref, cos_ref, sin_ref, fh_ref, fl_ref, ih_ref, il_ref, *rest):
    out_ref = rest[-1]
    sections, groups, blocks, _, depth, chans = x_ref.shape
    frames = cos_ref.shape[1]

    def dot(a, b):
        return jnp.dot(a, b, preferred_element_type=jnp.float32)

    for block in range(blocks):
        span = pl.ds(block * chans, chans)
        x = x_ref[:, :, block, 0].reshape(sections * groups * depth, chans)
        spec = dot(fh_ref[...], x) + dot(fl_ref[...], x)
        cosine = cos_ref[0, :, span]
        sine = sin_ref[0, :, span]
        real = spec[:frames] * cosine - spec[frames:] * sine
        imag = spec[:frames] * sine + spec[frames:] * cosine
        turned = jnp.concatenate((real, imag), axis=0)
        high = turned.astype(jnp.bfloat16)
        low = (turned - high.astype(jnp.float32)).astype(jnp.bfloat16)
        y = dot(ih_ref[...], high) + dot(ih_ref[...], low) + dot(il_ref[...], high)
        out_ref[0, :, span] = y[:frames] * y[:frames] + y[frames:] * y[frames:]


def dedisperse(series, cosine, sine, matrices, chunk, chunks, partial):
    sections, groups, blocks, beams, depth, chans = series.shape
    frames = cosine.shape[1]
    wide = blocks * chans
    whole = [pl.BlockSpec(m.shape, lambda i: (0, 0)) for m in matrices]
    tables = pl.BlockSpec((1, frames, wide), lambda i: (i, 0, 0))
    earlier = [] if partial is None else [partial]
    return pl.pallas_call(
        dedisperse_kernel,
        grid=(beams,),
        in_specs=[
            pl.BlockSpec(
                (sections, groups, blocks, 1, depth, chans), lambda i: (0, 0, 0, i, 0, 0)
            ),
            tables,
            tables,
        ]
        + whole
        + [pl.BlockSpec(memory_space=pl.ANY) for _ in earlier],
        out_specs=pl.BlockSpec((1, frames, wide), lambda i: (i, 0, chunk)),
        out_shape=jax.ShapeDtypeStruct((beams, frames, wide * chunks), jnp.float32),
        input_output_aliases={7: 0} if earlier else {},
        cost_estimate=pl.CostEstimate(
            flops=beams * wide * 2 * frames * 2 * frames * 14,
            bytes_accessed=beams * wide * frames * 16,
            transcendentals=0,
        ),
        name="dedisperse",
    )(series, cosine, sine, *matrices, *earlier)


def body(voltages, station_map, beam_table, weight_table, dm_trial):
    section_index = lax.axis_index("section")
    dom_index = lax.axis_index("dom")
    sections = lax.axis_size("section")
    doms = lax.axis_size("dom")
    groups = 2
    peers = doms // groups
    group_index = dom_index // peers
    stations = voltages.shape[0]
    frames = voltages.shape[1]
    beams = beam_table.shape[0]
    chans = weight_table.shape[2]
    per_device = beams // (sections * doms)
    local = frames // sections
    rows_here = stations * local
    station_groups = [[g * peers + p for p in range(peers)] for g in range(groups)]

    swapped = lax.ppermute(weight_table, "dom", [(d, (d + peers) % doms) for d in range(doms)])
    block = lax.dynamic_slice_in_dim(voltages, section_index * local, local, 1)
    rows = block.reshape(rows_here, NFFT)

    held = stations * peers
    mine = lax.dynamic_slice_in_dim(station_map, group_index * held, held, 0)
    arrival = jnp.take(beam_table, mine, axis=1, mode="clip").T
    swapped, rows = lax.optimization_barrier((swapped, rows))

    column = jnp.arange(peers * 2 * chans, dtype=jnp.int32)
    column_chan = column // (2 * chans) * chans + column % chans
    is_imag = column // chans % 2 == 1

    owner = section_index * doms + dom_index
    trials = lax.dynamic_slice_in_dim(dm_trial, owner * per_device, per_device, 0)
    measure = (trials + 1).astype(jnp.float32) / NDM
    bins = jnp.arange(frames, dtype=jnp.int32)
    kappa = jnp.where(bins < frames // 2, bins, bins - frames).astype(jnp.float32)
    matrices = frame_matrices(frames, sections, groups)

    sent = []
    for chunk in range(groups):
        table = dft_columns(chunk * peers * chans + column_chan, is_imag)
        spectrum = lax.dot_general(
            table, rows, (((0,), (1,)), ((), ())), preferred_element_type=jnp.float32
        )
        spectrum = spectrum.astype(jnp.bfloat16).reshape(peers, 2 * chans, rows_here)
        sent.append(
            lax.all_to_all(
                spectrum,
                "dom",
                split_axis=0,
                concat_axis=0,
                axis_index_groups=station_groups,
                tiled=True,
            )
        )
    power = None
    for chunk in range(groups):
        owned_table = jnp.where(group_index == chunk, weight_table, swapped)
        lookup = owned_table.transpose(2, 0, 1).reshape(chans, 2 * NTAB).astype(jnp.float32)
        weights = station_weights(lookup, arrival)
        signal = sent[chunk].reshape(peers, 2, chans, stations, local)
        signal = signal.transpose(2, 1, 4, 0, 3).reshape(chans, 2 * local, held)
        series = form_beams(signal, weights).transpose(2, 1, 0)
        series = series.reshape(sections * doms, per_device, 2 * local, chans)
        owned = lax.all_to_all(
            series, ("section", "dom"), split_axis=0, concat_axis=0, tiled=True
        )
        owned = owned.reshape(sections, groups, peers, per_device, 2 * local, chans)
        channels = chunk * peers * chans + jnp.arange(peers * chans, dtype=jnp.int32)
        freq = 1.0 + channels.astype(jnp.float32) / CH
        spread = 1.0 / (freq * freq * freq)
        coeff = math.pi * measure[:, None] * spread[None, :]
        phase = coeff[:, None, :] * (kappa * kappa / frames)[None, :, None]
        power = dedisperse(
            owned, jnp.cos(phase), jnp.sin(phase), matrices, chunk, groups, power
        )
    return power


def solution(mesh):
    in_specs = (P("dom", None, None), P(), P(), P(None, None, "dom"), P())
    out_specs = P(("section", "dom"), None, None)
    return jax.shard_map(body, mesh=mesh, in_specs=in_specs, out_specs=out_specs, check_vma=False)
```

```python
import math

import jax
import jax.numpy as jnp
from jax import lax
from jax.experimental import pallas as pl
from jax.experimental.pallas import tpu as pltpu
from jax.sharding import PartitionSpec as P

NFFT = 2048
CH = 1024
NTAB = 64
NDM = 32
LANES = 128
TILE = 16


def phasor_rows(steps, channels):
    product = steps[:, None] * channels[None, :] % NFFT
    angle = product.astype(jnp.float32) * (2.0 * math.pi / NFFT)
    return jnp.cos(angle), jnp.sin(angle)


def dft_columns(channels, is_imag):
    fine = 64
    coarse = NFFT // fine
    cos_a, sin_a = phasor_rows(fine * jnp.arange(coarse, dtype=jnp.int32), channels)
    cos_b, sin_b = phasor_rows(jnp.arange(fine, dtype=jnp.int32), channels)
    first = jnp.where(is_imag[None, :], -sin_a, cos_a)
    second = jnp.where(is_imag[None, :], -cos_a, -sin_a)
    sample = jnp.arange(NFFT, dtype=jnp.int32).astype(jnp.float32)
    window = 0.5 - 0.5 * jnp.cos(sample * (2.0 * math.pi / NFFT))
    window = window.reshape(coarse, fine) / math.sqrt(NFFT)
    first, second, cos_b, sin_b, window = lax.optimization_barrier(
        (first, second, cos_b, sin_b, window)
    )
    values = first[:, None, :] * cos_b[None] + second[:, None, :] * sin_b[None]
    values = values * window[:, :, None]
    return values.astype(jnp.bfloat16).reshape(NFFT, channels.shape[0])


def split_bf16(values):
    high = lax.reduce_precision(values, 8, 7)
    return high.astype(jnp.bfloat16), (values - high).astype(jnp.bfloat16)


def frame_matrices(frames, sections, groups):
    index = jnp.arange(frames, dtype=jnp.int32)
    angle = (index[:, None] * index[None, :] % frames).astype(jnp.float32) * (
        2.0 * math.pi / frames
    )
    cosine = jnp.cos(angle)
    sine = jnp.sin(angle)
    local = frames // sections
    forward = jnp.stack((jnp.stack((cosine, sine), 1), jnp.stack((-sine, cosine), 1)), 0)
    forward = forward.reshape(2 * frames, 2, sections, local).transpose(0, 2, 1, 3)
    forward = jnp.broadcast_to(
        forward[:, :, None], (2 * frames, sections, groups, 2, local)
    ).reshape(2 * frames, groups * 2 * frames)
    inverse = jnp.stack((jnp.stack((cosine, -sine), 1), jnp.stack((sine, cosine), 1)), 0)
    inverse = inverse.reshape(2 * frames, 2 * frames) / frames
    return split_bf16(forward) + split_bf16(inverse)


def pick_lanes(entries, where):
    dims = lax.GatherDimensionNumbers(
        offset_dims=(),
        collapsed_slice_dims=(1,),
        start_index_map=(1,),
        operand_batching_dims=(0,),
        start_indices_batching_dims=(0,),
    )
    return lax.gather(
        entries,
        where[..., None],
        dims,
        slice_sizes=(1, 1),
        mode=lax.GatherScatterMode.PROMISE_IN_BOUNDS,
    )


def weight_kernel(table_ref, index_ref, out_ref):
    stations, beams = index_ref.shape
    count = table_ref.shape[0]
    for tile in range(stations // TILE):
        span = pl.ds(tile * TILE, TILE)
        for part in range(2):
            where = (index_ref[span, :] + part * NTAB).astype(jnp.int16)
            for chan in range(count):
                entry = table_ref[pl.ds(chan, 1), :].astype(jnp.bfloat16)
                picked = pick_lanes(jnp.broadcast_to(entry, (TILE, LANES)), where)
                out_ref[chan, span, pl.ds(part * beams, beams)] = picked


def station_weights(table, index):
    stations, beams = index.shape
    chans = table.shape[0]
    block = min(16, chans)
    return pl.pallas_call(
        weight_kernel,
        grid=(chans // block,),
        in_specs=[
            pl.BlockSpec((block, LANES), lambda i: (i, 0)),
            pl.BlockSpec((stations, beams), lambda i: (0, 0)),
        ],
        out_specs=pl.BlockSpec((block, stations, 2 * beams), lambda i: (i, 0, 0)),
        out_shape=jax.ShapeDtypeStruct((chans, stations, 2 * beams), jnp.bfloat16),
        cost_estimate=pl.CostEstimate(
            flops=0, bytes_accessed=chans * 2 * beams * stations * 5, transcendentals=0
        ),
        name="station_weights",
    )(table, index)


def beam_kernel(signal_ref, weight_ref, out_ref, rows_ref):
    peers, _, count, _ = signal_ref.shape
    groups = rows_ref.shape[0]
    shared = peers // groups
    stations = LANES // shared
    _, depth, beams = out_ref.shape
    half = depth // 2
    for group in range(groups):
        for part in range(2):
            for frame in range(half):
                pieces = [
                    signal_ref[group * shared + peer, part, :, pl.ds(frame * stations, stations)]
                    for peer in range(shared)
                ]
                piece = jnp.concatenate([p.astype(jnp.float32) for p in pieces], axis=1)
                at = pl.ds(part * half + frame, count, stride=depth)
                rows_ref[group, at, :] = piece
    for chan in range(count):
        span = pl.ds(chan * depth, depth)
        rows = jnp.concatenate([rows_ref[group, span, :] for group in range(groups)], axis=1)
        product = jnp.dot(
            rows.astype(jnp.bfloat16), weight_ref[chan], preferred_element_type=jnp.float32
        )
        real = product[:half, :beams] - product[half:, beams:]
        imag = product[half:, :beams] + product[:half, beams:]
        out_ref[chan, :half] = real.astype(jnp.bfloat16)
        out_ref[chan, half:] = imag.astype(jnp.bfloat16)


def form_beams(signal, weights):
    peers, _, chans, width = signal.shape
    _, held, beams = weights.shape
    beams = beams // 2
    depth = 2 * width * peers // held
    block = min(16, chans)
    return pl.pallas_call(
        beam_kernel,
        grid=(chans // block,),
        in_specs=[
            pl.BlockSpec((peers, 2, block, width), lambda i: (0, 0, i, 0)),
            pl.BlockSpec((block, held, 2 * beams), lambda i: (i, 0, 0)),
        ],
        out_specs=pl.BlockSpec((block, depth, beams), lambda i: (i, 0, 0)),
        out_shape=jax.ShapeDtypeStruct((chans, depth, beams), jnp.bfloat16),
        scratch_shapes=[pltpu.VMEM((held // LANES, block * depth, LANES), jnp.float32)],
        cost_estimate=pl.CostEstimate(
            flops=chans * depth * held * beams * 4,
            bytes_accessed=chans * held * beams * 6,
            transcendentals=0,
        ),
        name="form_beams",
    )(signal, weights)


def dedisperse_kernel(x_ref, cos_ref, sin_ref, fh_ref, fl_ref, ih_ref, il_ref, *rest):
    *earlier, out_ref = rest
    sections, groups, blocks, beams, depth, chans = x_ref.shape
    frames = cos_ref.shape[1]
    done = 0
    for ref in earlier:
        out_ref[:, :, pl.ds(done, ref.shape[2])] = ref[...]
        done += ref.shape[2]

    def dot(a, b):
        return jnp.dot(a, b, preferred_element_type=jnp.float32)

    for beam in range(beams):
        x = jnp.concatenate(
            [
                x_ref[:, :, block, beam].reshape(sections * groups * depth, chans)
                for block in range(blocks)
            ],
            axis=1,
        )
        spec = dot(fh_ref[...], x) + dot(fl_ref[...], x)
        cosine = cos_ref[beam]
        sine = sin_ref[beam]
        real = spec[:frames] * cosine - spec[frames:] * sine
        imag = spec[:frames] * sine + spec[frames:] * cosine
        turned = jnp.concatenate((real, imag), axis=0)
        high = turned.astype(jnp.bfloat16)
        low = (turned - high.astype(jnp.float32)).astype(jnp.bfloat16)
        y = dot(ih_ref[...], high) + dot(ih_ref[...], low) + dot(il_ref[...], high)
        power = y[:frames] * y[:frames] + y[frames:] * y[frames:]
        out_ref[beam, :, pl.ds(done, blocks * chans)] = power


def dedisperse(series, cosine, sine, matrices, earlier):
    _, _, blocks, beams, _, chans = series.shape
    frames = cosine.shape[1]
    wide = blocks * chans
    operands = (series, cosine, sine, *matrices, *earlier)
    total = wide + sum(part.shape[2] for part in earlier)
    return pl.pallas_call(
        dedisperse_kernel,
        in_specs=[pl.BlockSpec(memory_space=pltpu.VMEM) for _ in operands],
        out_specs=pl.BlockSpec(memory_space=pltpu.VMEM),
        out_shape=jax.ShapeDtypeStruct((beams, frames, total), jnp.float32),
        cost_estimate=pl.CostEstimate(
            flops=beams * wide * 2 * frames * 2 * frames * 14,
            bytes_accessed=beams * wide * frames * 16,
            transcendentals=0,
        ),
        compiler_params=pltpu.CompilerParams(vmem_limit_bytes=24 << 20),
        name="dedisperse",
    )(*operands)


def body(voltages, station_map, beam_table, weight_table, dm_trial):
    section_index = lax.axis_index("section")
    dom_index = lax.axis_index("dom")
    sections = lax.axis_size("section")
    doms = lax.axis_size("dom")
    groups = 2
    peers = doms // groups
    group_index = dom_index // peers
    stations = voltages.shape[0]
    frames = voltages.shape[1]
    beams = beam_table.shape[0]
    chans = weight_table.shape[2]
    per_device = beams // (sections * doms)
    local = frames // sections
    rows_here = stations * local
    station_groups = [[g * peers + p for p in range(peers)] for g in range(groups)]

    swapped = lax.ppermute(weight_table, "dom", [(d, (d + peers) % doms) for d in range(doms)])
    block = lax.dynamic_slice_in_dim(voltages, section_index * local, local, 1)
    rows = block.transpose(1, 0, 2).reshape(rows_here, NFFT)

    held = stations * peers
    mine = lax.dynamic_slice_in_dim(station_map, group_index * held, held, 0)
    arrival = jnp.take(beam_table, mine, axis=1, mode="clip").T

    column = jnp.arange(peers * 2 * chans, dtype=jnp.int32)
    column_chan = column // (2 * chans) * chans + column % chans
    is_imag = column // chans % 2 == 1

    owner = section_index * doms + dom_index
    trials = lax.dynamic_slice_in_dim(dm_trial, owner * per_device, per_device, 0)
    measure = (trials + 1).astype(jnp.float32) / NDM
    bins = jnp.arange(frames, dtype=jnp.int32)
    kappa = jnp.where(bins < frames // 2, bins, bins - frames).astype(jnp.float32)
    matrices = frame_matrices(frames, sections, groups)

    sent = []
    for chunk in range(groups):
        table = dft_columns(chunk * peers * chans + column_chan, is_imag)
        spectrum = lax.dot_general(
            table, rows, (((0,), (1,)), ((), ())), preferred_element_type=jnp.float32
        )
        spectrum = spectrum.astype(jnp.bfloat16).reshape(peers, 2 * chans, rows_here)
        if chunk == 1:
            swapped, spectrum = lax.optimization_barrier((swapped, spectrum))
        sent.append(
            lax.all_to_all(
                spectrum,
                "dom",
                split_axis=0,
                concat_axis=0,
                axis_index_groups=station_groups,
                tiled=True,
            )
        )
    power = []
    for chunk in range(groups):
        owned_table = jnp.where(group_index == chunk, weight_table, swapped)
        lookup = owned_table.transpose(2, 0, 1).reshape(chans, 2 * NTAB).astype(jnp.float32)
        weights = station_weights(lookup, arrival)
        signal = sent[chunk].reshape(peers, 2, chans, rows_here)
        series = form_beams(signal, weights).transpose(2, 1, 0)
        series = series.reshape(sections * doms, per_device, 2 * local, chans)
        owned = lax.all_to_all(
            series, ("section", "dom"), split_axis=0, concat_axis=0, tiled=True
        )
        owned = owned.reshape(sections, groups, peers, per_device, 2 * local, chans)
        channels = chunk * peers * chans + jnp.arange(peers * chans, dtype=jnp.int32)
        freq = 1.0 + channels.astype(jnp.float32) / CH
        spread = 1.0 / (freq * freq * freq)
        coeff = math.pi * measure[:, None] * spread[None, :]
        phase = coeff[:, None, :] * (kappa * kappa / frames)[None, :, None]
        cosine = jnp.cos(phase)
        sine = jnp.sin(phase)
        power = [dedisperse(owned, cosine, sine, matrices, power)]
    return power[0]


def solution(mesh):
    in_specs = (P("dom", None, None), P(), P(), P(None, None, "dom"), P())
    out_specs = P(("section", "dom"), None, None)
    return jax.shard_map(body, mesh=mesh, in_specs=in_specs, out_specs=out_specs, check_vma=False)
```
